32 devices in a mesh: grp: 2 (over y), seq: 8 (over z, x), tp: 2 (over core).
Axes of the slice: x: 2, y: 2, z: 4, core: 2. Of those that a mesh axis runs over, the one named last changes fastest.
Arguments:
- queries: bfloat16 [4096, 2048], P(('grp', 'seq'), 'tp'), parts along dimension 0, may hold values from -9 to 9
- keys: bfloat16 [4096, 2048], P(('grp', 'seq'), 'tp'), parts along dimension 0, may hold values from -9 to 9
- values: bfloat16 [4096, 2048], P(('grp', 'seq'), 'tp'), parts along dimension 0, may hold values from -18 to 18
- segment_ids: int32 [4096], P(('grp', 'seq')), parts along dimension 0, may hold values from 0 to 7, never falling along the last dimension, each value on 1 to 512 neighbouring positions
- modality: int32 [4096], P(('grp', 'seq')), parts along dimension 0, may hold values 0 or 1
- norm_gain: float32 [2, 2048], P(None, 'tp'), may hold values from 0.1 to 1.9
Outputs:
- blended: bfloat16 [4096, 2048], P(('grp', 'seq'), 'tp'), parts along dimension 0
The draws below stay inside these ranges and needn't reach their ends.
There are 2 independent parts, one for each index of `grp`. The reference program is written for one: setup_inputs(seed, part) draws one part's arguments, and reference() takes and returns one part's arrays. A program takes and returns all parts, laid end to end along the dimension named above; an argument that names none is the same for every part. Nothing has to cross between parts.
Inputs may be any that keep to these rules, and one draw needn't show every extreme that they name: `segment_ids`: ids never fall along the sequence; each document holds 1 to 512 tokens, and one holds exactly that many.
All inputs are finite; a program needn't handle non-finite values. No bound on the sum of `modality` on one device may be relied on, other than what follows from the above.
Results may differ from the reference program's by a relative error of at most 0.009.
Values may be sent and summed in bfloat16 or wider, within the bound.
No kernel may reach another device: no remote copies, remote signals or barrier semaphores. Data moves between devices by JAX's collectives and lax.ppermute only.
A program may use at most 64 MiB of HBM per device.

```python
import math
import jax
import jax.numpy as jnp
import numpy as np
from jax import lax

HEADS = 16
HEAD_DIM = 128
TOK_DEV = 256
REACH = 2
TOKENS = 2048
DOCS = 8
N_SEQ = 8


def draw_entries(key, part):
    key_base = jax.random.fold_in(key, 7)
    key_query, key_other = jax.random.split(key_base, 2)
    array_shape = (TOKENS, HEADS * HEAD_DIM)
    query_draw = jnp.clip(jax.random.normal(key_query, array_shape, jnp.float32), -6.0, 6.0)
    key_draw = jnp.clip(jax.random.normal(key_other, array_shape, jnp.float32), -6.0, 6.0)
    return (query_draw, key_draw)


def draw_queries(key, part):
    return draw_entries(key, part)[0].astype(jnp.bfloat16)


def draw_keys(key, part):
    return draw_entries(key, part)[1].astype(jnp.bfloat16)


def draw_values(key, part):
    key_base = jax.random.fold_in(key, 11)
    key_entry, key_scale = jax.random.split(key_base, 2)
    array_shape = (TOKENS, HEADS * HEAD_DIM)
    entries = jnp.clip(jax.random.normal(key_entry, array_shape, jnp.float32), -6.0, 6.0)
    head_scale = jnp.exp(jax.random.uniform(key_scale, (HEADS,), jnp.float32, jnp.log(0.3), jnp.log(3.0)))
    column_scale = jnp.repeat(head_scale, HEAD_DIM)
    return (entries * column_scale[None, :]).astype(jnp.bfloat16)


def touch_ends(values, key, low, largest):
    place = [jax.random.randint(jax.random.fold_in(key, axis), (), 0, length) for axis, length in enumerate(values.shape)]
    main_axis = values.shape.index(max(values.shape))
    beside = place[:main_axis] + [(place[main_axis] + 1) % values.shape[main_axis]] + place[main_axis + 1:]
    return values.at[tuple(place)].set(low).at[tuple(beside)].set(largest)


def profile(number_of, total, limit, slope):
    weights = [(1 << 20) // math.isqrt(grade ** slope) + 1 for grade in range(2, number_of + 1)]
    spare, holding = total - limit - (number_of - 1), [1] * (number_of - 1)
    while spare > 0:
        candidates = [i for i in range(number_of - 1) if holding[i] < limit]
        pool, left = sum([weights[i] for i in candidates]), spare
        for i in candidates:
            extra = min(limit - holding[i], max(1, left * weights[i] // pool), spare)
            holding[i] = holding[i] + extra
            spare = spare - extra
    return np.array([limit] + holding)


def uneven(stream_key, count, total, bound, slope):
    if count == 2:
        one = jax.random.randint(stream_key, (), max(1, total - bound), min(bound, total - 1) + 1)
        return jnp.stack([one, total - one])
    tallies = jnp.asarray(profile(count, total, bound, slope), jnp.int32)
    pairs = (count - 1) // 2
    source_of, receiver = tallies[1:1 + 2 * pairs:2], tallies[2:2 + 2 * pairs:2]
    room = jnp.minimum(source_of - 1, bound - receiver)
    shifted = jax.random.randint(jax.random.fold_in(stream_key, 1), (pairs,), 0, 1 << 20) % (room + 1)
    tallies = tallies.at[1:1 + 2 * pairs:2].set(source_of - shifted).at[2:2 + 2 * pairs:2].set(receiver + shifted)
    return tallies[jax.random.permutation(jax.random.fold_in(stream_key, 2), count)]


def setup_inputs(seed: int = 0, part: int = 0) -> dict:
    streams_of = jax.random.split(jax.random.key(seed), 7)
    own_keys = jax.random.split(jax.random.fold_in(streams_of[6], part), 7)
    return {
        "queries": draw_queries(jax.random.fold_in(jax.random.fold_in(streams_of[6], part), 71), part),
        "keys": draw_keys(jax.random.fold_in(jax.random.fold_in(streams_of[6], part), 71), part),
        "values": draw_values(jax.random.fold_in(jax.random.fold_in(streams_of[6], part), 71), part),
        "segment_ids": jnp.searchsorted(jnp.cumsum(uneven(own_keys[3], DOCS, TOKENS, REACH * TOK_DEV, 1)), jnp.arange(TOKENS), side="right").astype(jnp.int32),
        "modality": touch_ends((jax.random.randint(own_keys[4], (TOKENS,), 0, 2) < 1).astype(jnp.int32), jax.random.fold_in(own_keys[4], 1), 0, 1),
        "norm_gain": jnp.clip(1.0 + 0.18 * jax.random.normal(streams_of[5], (2, HEADS * HEAD_DIM), jnp.float32), 0.1, 1.9),
    }


def attend_block(block_index, queries, keys, values, segment_ids):
    key_span = (REACH + 1) * TOK_DEV
    first_key = (jnp.maximum(block_index - REACH, 0) * TOK_DEV).astype(jnp.int32)
    first_query = (block_index * TOK_DEV).astype(jnp.int32)
    q_rows = lax.dynamic_slice_in_dim(queries, first_query, TOK_DEV, 0).astype(jnp.float32).reshape(TOK_DEV, HEADS, HEAD_DIM)
    k_rows = lax.dynamic_slice_in_dim(keys, first_key, key_span, 0).astype(jnp.float32).reshape(key_span, HEADS, HEAD_DIM)
    v_rows = lax.dynamic_slice_in_dim(values, first_key, key_span, 0).astype(jnp.float32).reshape(key_span, HEADS, HEAD_DIM)
    query_segs = lax.dynamic_slice_in_dim(segment_ids, first_query, TOK_DEV, 0)
    key_segs = lax.dynamic_slice_in_dim(segment_ids, first_key, key_span, 0)
    query_pos = first_query + jnp.arange(TOK_DEV, dtype=jnp.int32)
    key_pos = first_key + jnp.arange(key_span, dtype=jnp.int32)
    allowed = (query_segs[:, None] == key_segs[None, :]) & (key_pos[None, :] <= query_pos[:, None])
    scores = jnp.einsum('qhd,khd->hqk', q_rows, k_rows) * HEAD_DIM ** (-0.5)
    scores = jnp.where(allowed[None], scores, -jnp.inf)
    row_max = lax.optimization_barrier(jnp.max(scores, axis=2, keepdims=True))
    weights = jnp.exp(scores - row_max)
    row_total = lax.optimization_barrier(jnp.sum(weights, axis=2))
    rounded = weights.astype(jnp.bfloat16).astype(jnp.float32)
    summed = jnp.einsum('hqk,khd->qhd', rounded, v_rows)
    attended = summed / jnp.transpose(row_total)[:, :, None]
    return attended.reshape(TOK_DEV, HEADS * HEAD_DIM).astype(jnp.bfloat16)

def reference(queries, keys, values, segment_ids, modality, norm_gain):
    indices = jnp.arange(N_SEQ, dtype=jnp.int32)
    attended = lax.map(lambda block_index: attend_block(block_index, queries, keys, values, segment_ids), indices)
    attended = attended.reshape(TOKENS, HEADS * HEAD_DIM).astype(jnp.float32)
    mean_square = lax.optimization_barrier(jnp.sum(attended * attended, axis=1)) / (HEADS * HEAD_DIM)
    gain_rows = jnp.where((modality == 1)[:, None], norm_gain[1][None, :], norm_gain[0][None, :])
    blended = attended * lax.rsqrt(mean_square + 1e-05)[:, None] * gain_rows
    return blended.astype(jnp.bfloat16)
```

```python
import functools
import math

import jax
import jax.numpy as jnp
from jax import lax
from jax.experimental import pallas as pl
from jax.experimental.pallas import tpu as pltpu
from jax.sharding import PartitionSpec as P


HEAD_DIM = 128
CHUNKS = 4
SEG_ROWS = 16
NEG = -1e30
EPS = 1e-05


def column(row):
    return jnp.transpose(jnp.broadcast_to(row, (128, row.shape[1])))


def lanes(col, width):
    return jnp.concatenate([col] * (width // 128), axis=1)


def allowed_masks(me, own_seg, near_seg, far_seg):
    tok = own_seg.shape[1]
    q_seg = lanes(column(own_seg), tok)
    q_pos = lax.broadcasted_iota(jnp.int32, (tok, tok), 0)
    k_pos = lax.broadcasted_iota(jnp.int32, (tok, tok), 1)
    near_seg = jnp.where(me >= 1, near_seg, -1.0)
    far_seg = jnp.where(me >= 2, far_seg, -1.0)
    own = (q_seg == own_seg) & (k_pos <= q_pos)
    return own, q_seg == near_seg, q_seg == far_seg


def attend_head(q, keys, values, masks):
    factor = HEAD_DIM ** (-0.5) * math.log2(math.e)
    scores = []
    for key, mask in zip(keys, masks):
        s = lax.dot_general(q, key, (((1,), (1,)), ((), ())), preferred_element_type=jnp.float32)
        scores.append(jnp.where(mask, s, NEG))
    top = functools.reduce(jnp.maximum, scores)
    top = jnp.max(top, axis=1, keepdims=True) * factor
    weights = [jnp.exp2(s * factor - top) for s in scores]
    total = jnp.sum(functools.reduce(jnp.add, weights), axis=1, keepdims=True)
    acc = sum(
        lax.dot_general(w.astype(jnp.bfloat16), v, (((1,), (0,)), ((), ())), preferred_element_type=jnp.float32)
        for w, v in zip(weights, values)
    )
    return (acc / total).astype(jnp.bfloat16)


def attend_kernel(last, me_ref, *refs):
    q_ref, k_ref, v_ref, seg_ref, near_seg_ref, far_seg_ref = refs[:6]
    me = me_ref[0]
    tok, width = q_ref.shape
    seg = seg_ref[...].astype(jnp.float32)
    near_seg = near_seg_ref[...][0:1, :tok].astype(jnp.float32)
    far_seg = far_seg_ref[...][0:1, :tok].astype(jnp.float32)
    masks = allowed_masks(me, seg, near_seg, far_seg)
    if last:
        s_ref, f_ref, a_ref, p0, p1, p2 = refs[6:12]
        att_ref, sq_ref = refs[12:]
        odd = lax.rem(me, 2) == 1
        near = jnp.where(odd, s_ref[...], f_ref[...])
        far = jnp.where(odd, f_ref[...], a_ref[...])
    else:
        near_ref, far_ref = refs[6:8]
        att_ref, sq_ref = refs[8:]
        near, far = near_ref[:tok, :], far_ref[:tok, :]
    squares = None
    for h in range(width // HEAD_DIM):
        ks = slice(h * HEAD_DIM, (h + 1) * HEAD_DIM)
        vs = slice(width + h * HEAD_DIM, width + (h + 1) * HEAD_DIM)
        att = attend_head(
            q_ref[:, ks], (k_ref[:, ks], near[:, ks], far[:, ks]), (v_ref[:, ks], near[:, vs], far[:, vs]), masks
        )
        att_ref[:, ks] = att
        att = att.astype(jnp.float32)
        squares = att * att if squares is None else squares + att * att
    if last:
        squares = jnp.transpose(squares + p0[...] + p1[...] + p2[...])
        sq_ref[...] = jnp.sum(squares.reshape(squares.shape[0] // 8, 8, tok), axis=0)
    else:
        sq_ref[...] = squares


def finish_kernel(features, mine_ref, other_ref, mod_ref, gain_ref, *refs):
    att_refs, out_ref = refs[:-1], refs[-1]
    total = jnp.sum(mine_ref[...] + other_ref[...], axis=0, keepdims=True)
    inverse = column(lax.rsqrt(total / features + EPS))
    image = column(mod_ref[...].astype(jnp.float32)) == 1.0
    for c, att_ref in enumerate(att_refs):
        width = att_ref.shape[1]
        for b in range(width // 128):
            at = c * width + b * 128
            gain = jnp.where(image, gain_ref[1:2, at : at + 128], gain_ref[0:1, at : at + 128])
            att = att_ref[:, b * 128 : (b + 1) * 128].astype(jnp.float32)
            out_ref[:, at : at + 128] = (att * inverse * gain).astype(jnp.bfloat16)


def on_device(queries, keys, values, segment_ids, modality, norm_gain):
    tok, feat = queries.shape
    n = lax.axis_size("seq")
    me = lax.axis_index("seq")
    odd = (me % 2) == 1
    width = feat // CHUNKS
    ring2 = [(i, (i + 2) % n) for i in range(n)]
    shift2 = [(i, i + 2) for i in range(n - 2)]
    pair = [(i, i ^ 1) for i in range(n)]

    def send(value, pairs):
        return lax.ppermute(value, "seq", pairs)

    seg_row = segment_ids.astype(jnp.bfloat16)
    seg_block = jnp.pad(seg_row[None, :], ((0, SEG_ROWS - 1), (0, 2 * width - tok)))
    chunk = []
    for c in range(CHUNKS):
        cols = slice(c * width, (c + 1) * width)
        chunk.append(jnp.concatenate([keys[:, cols], values[:, cols]], axis=1))
    chunk[0] = jnp.concatenate([chunk[0], seg_block], axis=0)
    a0 = send(chunk[0], ring2)
    s = send(chunk[3], pair)
    a1 = send(chunk[1], ring2)
    a2 = send(chunk[2], ring2)
    x0 = send(jnp.where(odd, a0, chunk[0]), pair)
    f = send(jnp.where(odd, chunk[3], s), ring2)
    x1 = send(jnp.where(odd, a1, chunk[1]), pair)
    a3 = send(chunk[3], shift2)
    x2 = send(jnp.where(odd, a2, chunk[2]), pair)

    seg2d = segment_ids[None, :]
    me1 = me.astype(jnp.int32)[None]
    smem = pl.BlockSpec(memory_space=pltpu.SMEM)
    whole = lambda a: pl.BlockSpec(a.shape, lambda i: (0,) * len(a.shape))
    segs = pl.BlockSpec((SEG_ROWS, 2 * width), lambda i: (tok // SEG_ROWS, 0))
    flops = 3 * 4 * tok * tok * width

    def attend(c, last, rest):
        cols = pl.BlockSpec((tok, width), lambda i: (0, c))
        sq_shape = (8, tok) if last else (tok, 128)
        outs = (jax.ShapeDtypeStruct((tok, width), jnp.bfloat16), jax.ShapeDtypeStruct(sq_shape, jnp.float32))
        return pl.pallas_call(
            functools.partial(attend_kernel, last),
            grid=(1,),
            out_shape=outs,
            out_specs=tuple(whole(o) for o in outs),
            in_specs=[smem, cols, cols, cols, whole(seg2d), segs, segs] + [whole(r) for r in rest],
            name="attend_last" if last else "attend",
            cost_estimate=pl.CostEstimate(flops=flops, bytes_accessed=tok * width * 20, transcendentals=3 * tok * tok * 2),
        )(me1, queries, keys, values, seg2d, x0, a0, *rest)

    att, sq = [], []
    for c, (near, far) in enumerate(((x0, a0), (x1, a1), (x2, a2))):
        o, q = attend(c, False, (near, far))
        att.append(o)
        sq.append(q)
    o, q = attend(3, True, (s, f, a3, *sq))
    att.append(o)
    tp = lax.axis_size("tp")
    other = lax.ppermute(q, "tp", [(i, i ^ 1) for i in range(tp)])
    return pl.pallas_call(
        functools.partial(finish_kernel, float(feat * tp)),
        out_shape=jax.ShapeDtypeStruct((tok, feat), jnp.bfloat16),
        name="finish",
    )(q, other, modality[None, :], norm_gain, *att)


def solution(mesh):
    return jax.shard_map(
        on_device,
        mesh=mesh,
        in_specs=(
            P(("grp", "seq"), "tp"),
            P(("grp", "seq"), "tp"),
            P(("grp", "seq"), "tp"),
            P(("grp", "seq")),
            P(("grp", "seq")),
            P(None, "tp"),
        ),
        out_specs=P(("grp", "seq"), "tp"),
        check_vma=False,
    )
```

```python
import functools
import math

import jax
import jax.numpy as jnp
from jax import lax
from jax.experimental import pallas as pl
from jax.experimental.pallas import tpu as pltpu
from jax.sharding import PartitionSpec as P


HEAD_DIM = 128
CHUNKS = 4
SEG_ROWS = 16
NEG = -1e30
EPS = 1e-05
VMEM_LIMIT = 12 * 1024 * 1024


def column(row):
    return jnp.transpose(jnp.broadcast_to(row, (128, row.shape[1])))


def lanes(col, width):
    return jnp.concatenate([col] * (width // 128), axis=1)


def allowed_masks(me, own_seg, near_seg, far_seg):
    tok = own_seg.shape[1]
    q_seg = lanes(column(own_seg), tok)
    q_pos = lax.broadcasted_iota(jnp.int32, (tok, tok), 0)
    k_pos = lax.broadcasted_iota(jnp.int32, (tok, tok), 1)
    near_seg = jnp.where(me >= 1, near_seg, -1.0)
    far_seg = jnp.where(me >= 2, far_seg, -1.0)
    own = (q_seg == own_seg) & (k_pos <= q_pos)
    return own, q_seg == near_seg, q_seg == far_seg


def attend_head(q, keys, values, masks):
    factor = HEAD_DIM ** (-0.5) * math.log2(math.e)
    scores = []
    for key, mask in zip(keys, masks):
        s = lax.dot_general(q, key, (((1,), (1,)), ((), ())), preferred_element_type=jnp.float32)
        scores.append(jnp.where(mask, s, NEG))
    top = functools.reduce(jnp.maximum, scores)
    top = jnp.max(top, axis=1, keepdims=True) * factor
    weights = [jnp.exp2(s * factor - top) for s in scores]
    total = jnp.sum(functools.reduce(jnp.add, weights), axis=1, keepdims=True)
    acc = sum(
        lax.dot_general(w.astype(jnp.bfloat16), v, (((1,), (0,)), ((), ())), preferred_element_type=jnp.float32)
        for w, v in zip(weights, values)
    )
    return (acc / total).astype(jnp.bfloat16)


def pack_kernel(me_ref, keys_ref, values_ref, seg_ref, mod_ref, chunk_ref, aux_ref, ids_ref, sem):
    tok, width = keys_ref.shape[0], keys_ref.shape[1] // CHUNKS
    copies = [
        pltpu.make_async_copy(seg_ref, ids_ref.at[0], sem.at[0]),
        pltpu.make_async_copy(mod_ref, ids_ref.at[1], sem.at[1]),
        pltpu.make_async_copy(keys_ref.at[:, 0:width], chunk_ref.at[0:tok, 0:width], sem.at[2]),
        pltpu.make_async_copy(values_ref.at[:, 0:width], chunk_ref.at[0:tok, width : 2 * width], sem.at[3]),
    ]
    for copy in copies:
        copy.start()
    copies[0].wait()
    copies[1].wait()
    seg = ids_ref[0].astype(jnp.float32)
    mod = ids_ref[1].astype(jnp.float32)
    aux_ref[0:1, :] = seg
    aux_ref[1:2, :] = mod
    aux_ref[2:8, :] = jnp.zeros((6, tok), jnp.float32)
    chunk_ref[tok : tok + SEG_ROWS, 0:tok] = jnp.broadcast_to(seg, (SEG_ROWS, tok)).astype(jnp.bfloat16)
    chunk_ref[tok : tok + SEG_ROWS, tok:] = jnp.zeros((SEG_ROWS, 2 * width - tok), jnp.bfloat16)
    copies[2].wait()
    copies[3].wait()


def pack_rest_kernel(keys_ref, values_ref, *refs):
    chunk_refs, sem = refs[:-1], refs[-1]
    width = keys_ref.shape[1] // CHUNKS
    copies = []
    for c, chunk_ref in enumerate(chunk_refs, 1):
        cols = slice(c * width, (c + 1) * width)
        copies.append(pltpu.make_async_copy(keys_ref.at[:, cols], chunk_ref.at[:, 0:width], sem.at[2 * c - 2]))
        copies.append(
            pltpu.make_async_copy(values_ref.at[:, cols], chunk_ref.at[:, width : 2 * width], sem.at[2 * c - 1])
        )
    for copy in copies:
        copy.start()
    for copy in copies:
        copy.wait()


def attend_kernel(c, last, me_ref, *refs):
    q_ref, own_ref, aux_ref, near_seg_ref, far_seg_ref = refs[:5]
    me = me_ref[0]
    tok, width = q_ref.shape[0], q_ref.shape[1] // CHUNKS
    near_seg = near_seg_ref[tok : tok + SEG_ROWS, :tok][0:1, :].astype(jnp.float32)
    far_seg = far_seg_ref[tok : tok + SEG_ROWS, :tok][0:1, :].astype(jnp.float32)
    masks = allowed_masks(me, aux_ref[0:1, :], near_seg, far_seg)
    if last:
        s_ref, f_ref, a_ref, p0, p1, p2 = refs[5:11]
        att_ref, sq_ref = refs[11:]
        odd = lax.rem(me, 2) == 1
        near = jnp.where(odd, s_ref[...], f_ref[...])
        far = jnp.where(odd, f_ref[...], a_ref[...])
    else:
        near_ref, far_ref = refs[5:7]
        att_ref, sq_ref = refs[7:]
        near, far = near_ref[:tok, :], far_ref[:tok, :]
    squares = None
    for h in range(width // HEAD_DIM):
        ks = slice(h * HEAD_DIM, (h + 1) * HEAD_DIM)
        vs = slice(width + h * HEAD_DIM, width + (h + 1) * HEAD_DIM)
        own = slice(c * width + h * HEAD_DIM, c * width + (h + 1) * HEAD_DIM)
        att = attend_head(
            q_ref[:, own],
            (own_ref[:tok, ks], near[:, ks], far[:, ks]),
            (own_ref[:tok, vs], near[:, vs], far[:, vs]),
            masks,
        )
        att_ref[:, ks] = att
        att = att.astype(jnp.float32)
        squares = att * att if squares is None else squares + att * att
    if last:
        squares = jnp.transpose(squares + p0[...] + p1[...] + p2[...])
        sq_ref[...] = jnp.sum(squares.reshape(squares.shape[0] // 8, 8, tok), axis=0)
    else:
        sq_ref[...] = squares


def finish_kernel(features, mine_ref, other_ref, aux_ref, gain_ref, *refs):
    att_refs, out_ref = refs[:-1], refs[-1]
    total = jnp.sum(mine_ref[...] + other_ref[...], axis=0, keepdims=True)
    inverse = column(lax.rsqrt(total / features + EPS))
    image = column(aux_ref[1:2, :]) == 1.0
    for c, att_ref in enumerate(att_refs):
        width = att_ref.shape[1]
        for b in range(width // 128):
            at = c * width + b * 128
            gain = jnp.where(image, gain_ref[1:2, at : at + 128], gain_ref[0:1, at : at + 128])
            att = att_ref[:, b * 128 : (b + 1) * 128].astype(jnp.float32)
            out_ref[:, at : at + 128] = (att * inverse * gain).astype(jnp.bfloat16)


def on_device(queries, keys, values, segment_ids, modality, norm_gain):
    tok, feat = queries.shape
    n = lax.axis_size("seq")
    me = lax.axis_index("seq")
    odd = (me % 2) == 1
    width = feat // CHUNKS
    ring2 = [(i, (i + 2) % n) for i in range(n)]
    shift2 = [(i, i + 2) for i in range(n - 2)]
    pair = [(i, i ^ 1) for i in range(n)]

    def send(value, pairs):
        return lax.ppermute(value, "seq", pairs)

    def pick(at_odd, at_even):
        return jnp.where(odd, at_odd, at_even)

    smem = pl.BlockSpec(memory_space=pltpu.SMEM)
    vmem = pl.BlockSpec(memory_space=pltpu.VMEM)
    hbm = pl.BlockSpec(memory_space=pltpu.HBM)
    small = pltpu.CompilerParams(vmem_limit_bytes=VMEM_LIMIT)
    me1 = me.astype(jnp.int32)[None]
    first, aux = pl.pallas_call(
        pack_kernel,
        out_shape=(
            jax.ShapeDtypeStruct((tok + SEG_ROWS, 2 * width), jnp.bfloat16),
            jax.ShapeDtypeStruct((8, tok), jnp.float32),
        ),
        in_specs=[smem, hbm, hbm, hbm, hbm],
        out_specs=(vmem, vmem),
        scratch_shapes=[pltpu.VMEM((2, 1, tok), jnp.int32), pltpu.SemaphoreType.DMA((4,))],
        name="pack",
        compiler_params=small,
    )(me1, keys, values, segment_ids[None, :], modality[None, :])
    rest = pl.pallas_call(
        pack_rest_kernel,
        out_shape=tuple(jax.ShapeDtypeStruct((tok, 2 * width), jnp.bfloat16) for _ in range(CHUNKS - 1)),
        in_specs=[hbm, hbm],
        out_specs=(vmem,) * (CHUNKS - 1),
        scratch_shapes=[pltpu.SemaphoreType.DMA((2 * CHUNKS - 2,))],
        name="pack_rest",
        compiler_params=small,
    )(keys, values)
    chunk = (first, *rest)
    a0 = send(chunk[0], ring2)
    s = send(chunk[3], pair)
    a1 = send(chunk[1], ring2)
    a2 = send(chunk[2], ring2)
    x0 = send(pick(a0, chunk[0]), pair)
    f = send(pick(chunk[3], s), ring2)
    x1 = send(pick(a1, chunk[1]), pair)
    a3 = send(chunk[3], shift2)
    x2 = send(pick(a2, chunk[2]), pair)

    flops = 3 * 4 * tok * tok * width

    def attend(c, last, rest):
        sq_shape = (8, tok) if last else (tok, 128)
        outs = (jax.ShapeDtypeStruct((tok, width), jnp.bfloat16), jax.ShapeDtypeStruct(sq_shape, jnp.float32))
        return pl.pallas_call(
            functools.partial(attend_kernel, c, last),
            out_shape=outs,
            out_specs=(vmem, vmem),
            in_specs=[smem] + [vmem] * (5 + len(rest)),
            compiler_params=small,
            cost_estimate=pl.CostEstimate(flops=flops, bytes_accessed=tok * width * 20, transcendentals=3 * tok * tok * 2),
        )(me1, queries, chunk[c], aux, x0, a0, *rest)

    att, sq = [], []
    for c, (near, far) in enumerate(((x0, a0), (x1, a1), (x2, a2))):
        o, q = attend(c, False, (near, far))
        att.append(o)
        sq.append(q)
    o, q = attend(3, True, (s, f, a3, *sq))
    att.append(o)
    tp = lax.axis_size("tp")
    other = lax.ppermute(q, "tp", [(i, i ^ 1) for i in range(tp)])
    return pl.pallas_call(
        functools.partial(finish_kernel, float(feat * tp)),
        out_shape=jax.ShapeDtypeStruct((tok, feat), jnp.bfloat16),
        in_specs=[vmem] * (4 + CHUNKS),
        out_specs=vmem,
        name="finish",
        compiler_params=small,
    )(q, other, aux, norm_gain, *att)


def solution(mesh):
    return jax.shard_map(
        on_device,
        mesh=mesh,
        in_specs=(
            P(("grp", "seq"), "tp"),
            P(("grp", "seq"), "tp"),
            P(("grp", "seq"), "tp"),
            P(("grp", "seq")),
            P(("grp", "seq")),
            P(None, "tp"),
        ),
        out_specs=P(("grp", "seq"), "tp"),
        check_vma=False,
    )
```

```python
import functools
import math

import jax
import jax.numpy as jnp
from jax import lax
from jax.experimental import pallas as pl
from jax.experimental.pallas import tpu as pltpu
from jax.sharding import PartitionSpec as P


HEAD_DIM = 128
CHUNKS = 4
SEG_ROWS = 16
NEG = -1e30
EPS = 1e-05
FINISH_BLOCKS = 4
VMEM_LIMIT = 12 * 1024 * 1024


def column(row):
    return jnp.transpose(jnp.broadcast_to(row, (128, row.shape[1])))


def lanes(col, width):
    return jnp.concatenate([col] * (width // 128), axis=1)


def allowed_masks(me, own_seg, near_seg, far_seg):
    tok = own_seg.shape[1]
    q_seg = lanes(column(own_seg), tok)
    q_pos = lax.broadcasted_iota(jnp.int32, (tok, tok), 0)
    k_pos = lax.broadcasted_iota(jnp.int32, (tok, tok), 1)
    near_seg = jnp.where(me >= 1, near_seg, -1.0)
    far_seg = jnp.where(me >= 2, far_seg, -1.0)
    own = (q_seg == own_seg) & (k_pos <= q_pos)
    return own, q_seg == near_seg, q_seg == far_seg


def attend_head(q, keys, values, masks):
    factor = HEAD_DIM ** (-0.5) * math.log2(math.e)
    scores = []
    for key, mask in zip(keys, masks):
        s = lax.dot_general(q, key, (((1,), (1,)), ((), ())), preferred_element_type=jnp.float32)
        scores.append(jnp.where(mask, s, NEG))
    top = functools.reduce(jnp.maximum, scores)
    top = jnp.max(top, axis=1, keepdims=True) * factor
    weights = [jnp.exp2(s * factor - top) for s in scores]
    total = jnp.sum(functools.reduce(jnp.add, weights), axis=1, keepdims=True)
    acc = sum(
        lax.dot_general(w.astype(jnp.bfloat16), v, (((1,), (0,)), ((), ())), preferred_element_type=jnp.float32)
        for w, v in zip(weights, values)
    )
    return (acc / total).astype(jnp.bfloat16)


def pack_kernel(me_ref, keys_ref, values_ref, seg_ref, mod_ref, chunk_ref, aux_ref, ids_ref, sem):
    tok, width = keys_ref.shape[0], keys_ref.shape[1] // CHUNKS
    copies = [
        pltpu.make_async_copy(seg_ref, ids_ref.at[0], sem.at[0]),
        pltpu.make_async_copy(mod_ref, ids_ref.at[1], sem.at[1]),
        pltpu.make_async_copy(keys_ref.at[:, 0:width], chunk_ref.at[0:tok, 0:width], sem.at[2]),
        pltpu.make_async_copy(values_ref.at[:, 0:width], chunk_ref.at[0:tok, width : 2 * width], sem.at[3]),
    ]
    for copy in copies:
        copy.start()
    copies[0].wait()
    copies[1].wait()
    seg = ids_ref[0].astype(jnp.float32)
    mod = ids_ref[1].astype(jnp.float32)
    aux_ref[0:1, :] = seg
    aux_ref[1:2, :] = mod
    aux_ref[2:8, :] = jnp.zeros((6, tok), jnp.float32)
    chunk_ref[tok : tok + SEG_ROWS, 0:tok] = jnp.broadcast_to(seg, (SEG_ROWS, tok)).astype(jnp.bfloat16)
    chunk_ref[tok : tok + SEG_ROWS, tok:] = jnp.zeros((SEG_ROWS, 2 * width - tok), jnp.bfloat16)
    copies[2].wait()
    copies[3].wait()


def pack_rest_kernel(keys_ref, values_ref, *refs):
    chunk_refs, sem = refs[:-1], refs[-1]
    width = keys_ref.shape[1] // CHUNKS
    copies = []
    for c, chunk_ref in enumerate(chunk_refs, 1):
        cols = slice(c * width, (c + 1) * width)
        copies.append(pltpu.make_async_copy(keys_ref.at[:, cols], chunk_ref.at[:, 0:width], sem.at[2 * c - 2]))
        copies.append(
            pltpu.make_async_copy(values_ref.at[:, cols], chunk_ref.at[:, width : 2 * width], sem.at[2 * c - 1])
        )
    for copy in copies:
        copy.start()
    for copy in copies:
        copy.wait()


def attend_kernel(c, last, me_ref, *refs):
    q_ref, own_ref, aux_ref, near_seg_ref, far_seg_ref = refs[:5]
    me = me_ref[0]
    tok, width = q_ref.shape[0], q_ref.shape[1] // CHUNKS
    near_seg = near_seg_ref[tok : tok + SEG_ROWS, :tok][0:1, :].astype(jnp.float32)
    far_seg = far_seg_ref[tok : tok + SEG_ROWS, :tok][0:1, :].astype(jnp.float32)
    masks = allowed_masks(me, aux_ref[0:1, :], near_seg, far_seg)
    if last:
        s_ref, f_ref, a_ref, p0, p1, p2 = refs[5:11]
        att_ref, sq_ref = refs[11:]
        odd = lax.rem(me, 2) == 1
        near = jnp.where(odd, s_ref[...], f_ref[...])
        far = jnp.where(odd, f_ref[...], a_ref[...])
    else:
        near_ref, far_ref = refs[5:7]
        att_ref, sq_ref = refs[7:]
        near, far = near_ref[:tok, :], far_ref[:tok, :]
    squares = None
    for h in range(width // HEAD_DIM):
        ks = slice(h * HEAD_DIM, (h + 1) * HEAD_DIM)
        vs = slice(width + h * HEAD_DIM, width + (h + 1) * HEAD_DIM)
        own = slice(c * width + h * HEAD_DIM, c * width + (h + 1) * HEAD_DIM)
        att = attend_head(
            q_ref[:, own],
            (own_ref[:tok, ks], near[:, ks], far[:, ks]),
            (own_ref[:tok, vs], near[:, vs], far[:, vs]),
            masks,
        )
        att_ref[:, ks] = att
        att = att.astype(jnp.float32)
        squares = att * att if squares is None else squares + att * att
    if last:
        squares = jnp.transpose(squares + p0[...] + p1[...] + p2[...])
        sq_ref[...] = jnp.sum(squares.reshape(squares.shape[0] // 8, 8, tok), axis=0)
    else:
        sq_ref[...] = squares


def finish_kernel(features, mine_ref, other_ref, aux_ref, gain_ref, *refs):
    att_refs, (out_hbm, out_ref, sem) = refs[:-3], refs[-3:]
    tok = out_ref.shape[0]
    total = jnp.sum(mine_ref[...] + other_ref[...], axis=0, keepdims=True)
    inverse = column(lax.rsqrt(total / features + EPS))
    image = column(aux_ref[1:2, :]) == 1.0
    rows = tok // FINISH_BLOCKS
    copies = []
    for r in range(FINISH_BLOCKS):
        block = slice(r * rows, (r + 1) * rows)
        for c, att_ref in enumerate(att_refs):
            width = att_ref.shape[1]
            for b in range(width // 128):
                at = c * width + b * 128
                gain = jnp.where(image[block], gain_ref[1:2, at : at + 128], gain_ref[0:1, at : at + 128])
                att = att_ref[block, b * 128 : (b + 1) * 128].astype(jnp.float32)
                out_ref[block, at : at + 128] = (att * inverse[block] * gain).astype(jnp.bfloat16)
        copies.append(pltpu.make_async_copy(out_ref.at[block], out_hbm.at[block], sem.at[r]))
        copies[-1].start()
    for copy in copies:
        copy.wait()


def on_device(queries, keys, values, segment_ids, modality, norm_gain):
    tok, feat = queries.shape
    n = lax.axis_size("seq")
    me = lax.axis_index("seq")
    odd = (me % 2) == 1
    width = feat // CHUNKS
    ring2 = [(i, (i + 2) % n) for i in range(n)]
    shift2 = [(i, i + 2) for i in range(n - 2)]
    pair = [(i, i ^ 1) for i in range(n)]

    def send(value, pairs):
        return lax.ppermute(value, "seq", pairs)

    def pick(at_odd, at_even):
        return jnp.where(odd, at_odd, at_even)

    smem = pl.BlockSpec(memory_space=pltpu.SMEM)
    vmem = pl.BlockSpec(memory_space=pltpu.VMEM)
    hbm = pl.BlockSpec(memory_space=pltpu.HBM)
    in_hbm = lambda a: pltpu.with_memory_space_constraint(a, pltpu.HBM)
    small = pltpu.CompilerParams(vmem_limit_bytes=VMEM_LIMIT)
    me1 = me.astype(jnp.int32)[None]
    first, aux = pl.pallas_call(
        pack_kernel,
        out_shape=(
            jax.ShapeDtypeStruct((tok + SEG_ROWS, 2 * width), jnp.bfloat16),
            jax.ShapeDtypeStruct((8, tok), jnp.float32),
        ),
        in_specs=[smem, hbm, hbm, hbm, hbm],
        out_specs=(vmem, vmem),
        scratch_shapes=[pltpu.VMEM((2, 1, tok), jnp.int32), pltpu.SemaphoreType.DMA((4,))],
        name="pack",
        compiler_params=small,
    )(me1, in_hbm(keys), in_hbm(values), in_hbm(segment_ids[None, :]), in_hbm(modality[None, :]))
    rest = pl.pallas_call(
        pack_rest_kernel,
        out_shape=tuple(jax.ShapeDtypeStruct((tok, 2 * width), jnp.bfloat16) for _ in range(CHUNKS - 1)),
        in_specs=[hbm, hbm],
        out_specs=(vmem,) * (CHUNKS - 1),
        scratch_shapes=[pltpu.SemaphoreType.DMA((2 * CHUNKS - 2,))],
        name="pack_rest",
        compiler_params=small,
    )(in_hbm(keys), in_hbm(values))
    chunk = (first, *rest)
    a0 = send(chunk[0], ring2)
    s = send(chunk[3], pair)
    a1 = send(chunk[1], ring2)
    a2 = send(chunk[2], ring2)
    x0 = send(pick(a0, chunk[0]), pair)
    f = send(pick(chunk[3], s), ring2)
    x1 = send(pick(a1, chunk[1]), pair)
    a3 = send(chunk[3], shift2)
    x2 = send(pick(a2, chunk[2]), pair)

    flops = 3 * 4 * tok * tok * width

    def attend(c, last, rest):
        sq_shape = (8, tok) if last else (tok, 128)
        outs = (jax.ShapeDtypeStruct((tok, width), jnp.bfloat16), jax.ShapeDtypeStruct(sq_shape, jnp.float32))
        return pl.pallas_call(
            functools.partial(attend_kernel, c, last),
            out_shape=outs,
            out_specs=(vmem, vmem),
            in_specs=[smem] + [vmem] * (5 + len(rest)),
            compiler_params=small,
            cost_estimate=pl.CostEstimate(flops=flops, bytes_accessed=tok * width * 20, transcendentals=3 * tok * tok * 2),
        )(me1, queries, chunk[c], aux, x0, a0, *rest)

    att, sq = [], []
    for c, (near, far) in enumerate(((x0, a0), (x1, a1), (x2, a2))):
        o, q = attend(c, False, (near, far))
        att.append(o)
        sq.append(q)
    o, q = attend(3, True, (s, f, a3, *sq))
    att.append(o)
    tp = lax.axis_size("tp")
    other = lax.ppermute(q, "tp", [(i, i ^ 1) for i in range(tp)])
    return pl.pallas_call(
        functools.partial(finish_kernel, float(feat * tp)),
        out_shape=jax.ShapeDtypeStruct((tok, feat), jnp.bfloat16),
        in_specs=[vmem] * (4 + CHUNKS),
        out_specs=hbm,
        scratch_shapes=[pltpu.VMEM((tok, feat), jnp.bfloat16), pltpu.SemaphoreType.DMA((FINISH_BLOCKS,))],
        name="finish",
        compiler_params=small,
    )(q, other, aux, norm_gain, *att)


def solution(mesh):
    return jax.shard_map(
        on_device,
        mesh=mesh,
        in_specs=(
            P(("grp", "seq"), "tp"),
            P(("grp", "seq"), "tp"),
            P(("grp", "seq"), "tp"),
            P(("grp", "seq")),
            P(("grp", "seq")),
            P(None, "tp"),
        ),
        out_specs=P(("grp", "seq"), "tp"),
        check_vma=False,
    )
```

```python
import functools
import math

import jax
import jax.numpy as jnp
from jax import lax
from jax.experimental import pallas as pl
from jax.experimental.pallas import tpu as pltpu
from jax.sharding import PartitionSpec as P


HEAD_DIM = 128
CHUNKS = 4
FACTOR = HEAD_DIM ** (-0.5) * math.log2(math.e)
SEG_ROWS = 16
NEG = -1e30
EPS = 1e-05
FINISH_BLOCKS = 4
VMEM_LIMIT = 12 * 1024 * 1024


def column(row):
    return jnp.transpose(jnp.broadcast_to(row, (128, row.shape[1])))


def lanes(col, width):
    return jnp.concatenate([col] * (width // 128), axis=1)


def allowed_masks(me, own_seg, near_seg, far_seg):
    tok = own_seg.shape[1]
    q_seg = lanes(column(own_seg), tok)
    q_pos = lax.broadcasted_iota(jnp.int32, (tok, tok), 0)
    k_pos = lax.broadcasted_iota(jnp.int32, (tok, tok), 1)
    near_seg = jnp.where(me >= 1, near_seg, -1.0)
    far_seg = jnp.where(me >= 2, far_seg, -1.0)
    own = (q_seg == own_seg) & (k_pos <= q_pos)
    return own, q_seg == near_seg, q_seg == far_seg


def own_mask(own_seg):
    tok = own_seg.shape[1]
    q_pos = lax.broadcasted_iota(jnp.int32, (tok, tok), 0)
    k_pos = lax.broadcasted_iota(jnp.int32, (tok, tok), 1)
    return (lanes(column(own_seg), tok) == own_seg) & (k_pos <= q_pos)


def weigh(q, keys, masks):
    scores = []
    for key, mask in zip(keys, masks):
        s = lax.dot_general(q, key, (((1,), (1,)), ((), ())), preferred_element_type=jnp.float32)
        scores.append(jnp.where(mask, s, NEG))
    top = functools.reduce(jnp.maximum, scores)
    top = jnp.max(top, axis=1, keepdims=True) * FACTOR
    weights = [jnp.exp2(s * FACTOR - top) for s in scores]
    total = jnp.sum(functools.reduce(jnp.add, weights), axis=1, keepdims=True)
    return weights, top, total


def gather(weights, values):
    return sum(
        lax.dot_general(w.astype(jnp.bfloat16), v, (((1,), (0,)), ((), ())), preferred_element_type=jnp.float32)
        for w, v in zip(weights, values)
    )


def seg_of(ref, tok):
    return ref[tok : tok + SEG_ROWS, :tok][0:1, :].astype(jnp.float32)


def columns(width, h):
    return slice(h * HEAD_DIM, (h + 1) * HEAD_DIM), slice(width + h * HEAD_DIM, width + (h + 1) * HEAD_DIM)


def pack_kernel(me_ref, keys_ref, values_ref, seg_ref, mod_ref, chunk_ref, aux_ref, ids_ref, sem):
    tok, width = keys_ref.shape[0], keys_ref.shape[1] // CHUNKS
    copies = [
        pltpu.make_async_copy(seg_ref, ids_ref.at[0], sem.at[0]),
        pltpu.make_async_copy(mod_ref, ids_ref.at[1], sem.at[1]),
        pltpu.make_async_copy(keys_ref.at[:, 0:width], chunk_ref.at[0:tok, 0:width], sem.at[2]),
        pltpu.make_async_copy(values_ref.at[:, 0:width], chunk_ref.at[0:tok, width : 2 * width], sem.at[3]),
    ]
    for copy in copies:
        copy.start()
    copies[0].wait()
    copies[1].wait()
    seg = ids_ref[0].astype(jnp.float32)
    mod = ids_ref[1].astype(jnp.float32)
    aux_ref[0:1, :] = seg
    aux_ref[1:2, :] = mod
    aux_ref[2:8, :] = jnp.zeros((6, tok), jnp.float32)
    chunk_ref[tok : tok + SEG_ROWS, 0:tok] = jnp.broadcast_to(seg, (SEG_ROWS, tok)).astype(jnp.bfloat16)
    chunk_ref[tok : tok + SEG_ROWS, tok:] = jnp.zeros((SEG_ROWS, 2 * width - tok), jnp.bfloat16)
    copies[2].wait()
    copies[3].wait()


def pack_rest_kernel(keys_ref, values_ref, *refs):
    chunk_refs, sem = refs[:-1], refs[-1]
    width = keys_ref.shape[1] // CHUNKS
    copies = []
    for c, chunk_ref in enumerate(chunk_refs, 1):
        cols = slice(c * width, (c + 1) * width)
        copies.append(pltpu.make_async_copy(keys_ref.at[:, cols], chunk_ref.at[:, 0:width], sem.at[2 * c - 2]))
        copies.append(
            pltpu.make_async_copy(values_ref.at[:, cols], chunk_ref.at[:, width : 2 * width], sem.at[2 * c - 1])
        )
    for copy in copies:
        copy.start()
    for copy in copies:
        copy.wait()


def attend_kernel(c, me_ref, q_ref, own_ref, aux_ref, near_seg_ref, far_seg_ref, near_ref, far_ref, att_ref, sq_ref):
    me = me_ref[0]
    tok, width = q_ref.shape[0], q_ref.shape[1] // CHUNKS

    def attend(blocks, masks):
        squares = None
        for h in range(width // HEAD_DIM):
            ks, vs = columns(width, h)
            q = q_ref[:, c * width + h * HEAD_DIM : c * width + (h + 1) * HEAD_DIM]
            weights, _, total = weigh(q, [b[0:tok, ks] for b in blocks], masks)
            att = (gather(weights, [b[0:tok, vs] for b in blocks]) / total).astype(jnp.bfloat16)
            att_ref[:, ks] = att
            att = att.astype(jnp.float32)
            squares = att * att if squares is None else squares + att * att
        sq_ref[...] = squares

    @pl.when(me == 0)
    def _():
        attend([own_ref], [own_mask(aux_ref[0:1, :])])

    @pl.when(me > 0)
    def _():
        masks = allowed_masks(me, aux_ref[0:1, :], seg_of(near_seg_ref, tok), seg_of(far_seg_ref, tok))
        attend([own_ref, near_ref, far_ref], masks)


def partial_kernel(c, me_ref, q_ref, own_ref, aux_ref, near_seg_ref, far_seg_ref, s_ref, f_ref, acc_ref, stat_ref):
    me = me_ref[0]
    odd = lax.rem(me, 2) == 1
    tok, width = q_ref.shape[0], q_ref.shape[1] // CHUNKS

    def attend(blocks, masks):
        for h in range(width // HEAD_DIM):
            ks, vs = columns(width, h)
            q = q_ref[:, c * width + h * HEAD_DIM : c * width + (h + 1) * HEAD_DIM]
            weights, top, total = weigh(q, [b[0:tok, ks] for b in blocks], masks)
            acc_ref[:, ks] = gather(weights, [b[0:tok, vs] for b in blocks])
            stat_ref[2 * h] = jnp.broadcast_to(top, (tok, HEAD_DIM))
            stat_ref[2 * h + 1] = jnp.broadcast_to(total, (tok, HEAD_DIM))

    @pl.when(me == 0)
    def _():
        attend([own_ref], [own_mask(aux_ref[0:1, :])])

    @pl.when(me > 0)
    def _():
        masks = allowed_masks(me, aux_ref[0:1, :], seg_of(near_seg_ref, tok), seg_of(far_seg_ref, tok))

        @pl.when(odd)
        def _():
            attend([own_ref, s_ref, f_ref], masks)

        @pl.when(jnp.logical_not(odd))
        def _():
            attend([own_ref, f_ref], masks[:2])


def last_kernel(c, me_ref, q_ref, aux_ref, far_seg_ref, far_ref, acc_ref, stat_ref, p0, p1, p2, att_ref, sq_ref):
    me = me_ref[0]
    tok, width = q_ref.shape[0], q_ref.shape[1] // CHUNKS
    per = width // HEAD_DIM
    merge = jnp.logical_and(lax.rem(me, 2) == 0, me >= 2)

    def finish(parts):
        squares = p0[...] + p1[...] + p2[...]
        for h, att in enumerate(parts):
            att = att.astype(jnp.bfloat16)
            att_ref[:, columns(width, h)[0]] = att
            att = att.astype(jnp.float32)
            squares = squares + att * att
        squares = jnp.transpose(squares)
        sq_ref[...] = jnp.sum(squares.reshape(squares.shape[0] // 8, 8, tok), axis=0)

    @pl.when(jnp.logical_not(merge))
    def _():
        finish([acc_ref[:, columns(width, h)[0]] / stat_ref[2 * h + 1] for h in range(per)])

    @pl.when(merge)
    def _():
        mask = lanes(column(aux_ref[0:1, :]), tok) == seg_of(far_seg_ref, tok)
        parts = []
        for h in range(per):
            ks, vs = columns(width, h)
            q = q_ref[:, c * width + h * HEAD_DIM : c * width + (h + 1) * HEAD_DIM]
            s = lax.dot_general(q, far_ref[:, ks], (((1,), (1,)), ((), ())), preferred_element_type=jnp.float32)
            s = jnp.where(mask, s, NEG) * FACTOR
            old = stat_ref[2 * h]
            top = jnp.maximum(old, jnp.max(s, axis=1, keepdims=True))
            weights = jnp.exp2(s - lanes(top, tok))
            scale = jnp.exp2(old - top)
            total = stat_ref[2 * h + 1] * scale + jnp.sum(weights, axis=1, keepdims=True)
            parts.append((acc_ref[:, ks] * scale + gather([weights], [far_ref[:, vs]])) / total)
        finish(parts)


def finish_kernel(features, mine_ref, other_ref, aux_ref, gain_ref, *refs):
    att_refs, (out_hbm, out_ref, sem) = refs[:-3], refs[-3:]
    tok = out_ref.shape[0]
    total = jnp.sum(mine_ref[...] + other_ref[...], axis=0, keepdims=True)
    inverse = column(lax.rsqrt(total / features + EPS))
    image = column(aux_ref[1:2, :]) == 1.0
    rows = tok // FINISH_BLOCKS
    copies = []
    for r in range(FINISH_BLOCKS):
        block = slice(r * rows, (r + 1) * rows)
        for c, att_ref in enumerate(att_refs):
            width = att_ref.shape[1]
            for b in range(width // 128):
                at = c * width + b * 128
                gain = jnp.where(image[block], gain_ref[1:2, at : at + 128], gain_ref[0:1, at : at + 128])
                att = att_ref[block, b * 128 : (b + 1) * 128].astype(jnp.float32)
                out_ref[block, at : at + 128] = (att * inverse[block] * gain).astype(jnp.bfloat16)
        copies.append(pltpu.make_async_copy(out_ref.at[block], out_hbm.at[block], sem.at[r]))
        copies[-1].start()
    for copy in copies:
        copy.wait()


def on_device(queries, keys, values, segment_ids, modality, norm_gain):
    tok, feat = queries.shape
    n = lax.axis_size("seq")
    me = lax.axis_index("seq")
    odd = (me % 2) == 1
    width = feat // CHUNKS
    ring2 = [(i, (i + 2) % n) for i in range(n)]
    shift2 = [(i, i + 2) for i in range(n - 2)]
    pair = [(i, i ^ 1) for i in range(n)]

    def send(value, pairs):
        return lax.ppermute(value, "seq", pairs)

    def pick(at_odd, at_even):
        return jnp.where(odd, at_odd, at_even)

    smem = pl.BlockSpec(memory_space=pltpu.SMEM)
    vmem = pl.BlockSpec(memory_space=pltpu.VMEM)
    hbm = pl.BlockSpec(memory_space=pltpu.HBM)
    in_hbm = lambda a: pltpu.with_memory_space_constraint(a, pltpu.HBM)
    small = pltpu.CompilerParams(vmem_limit_bytes=VMEM_LIMIT)
    me1 = me.astype(jnp.int32)[None]
    first, aux = pl.pallas_call(
        pack_kernel,
        out_shape=(
            jax.ShapeDtypeStruct((tok + SEG_ROWS, 2 * width), jnp.bfloat16),
            jax.ShapeDtypeStruct((8, tok), jnp.float32),
        ),
        in_specs=[smem, hbm, hbm, hbm, hbm],
        out_specs=(vmem, vmem),
        scratch_shapes=[pltpu.VMEM((2, 1, tok), jnp.int32), pltpu.SemaphoreType.DMA((4,))],
        name="pack",
        compiler_params=small,
    )(me1, in_hbm(keys), in_hbm(values), in_hbm(segment_ids[None, :]), in_hbm(modality[None, :]))
    rest = pl.pallas_call(
        pack_rest_kernel,
        out_shape=tuple(jax.ShapeDtypeStruct((tok, 2 * width), jnp.bfloat16) for _ in range(CHUNKS - 1)),
        in_specs=[hbm, hbm],
        out_specs=(vmem,) * (CHUNKS - 1),
        scratch_shapes=[pltpu.SemaphoreType.DMA((2 * CHUNKS - 2,))],
        name="pack_rest",
        compiler_params=small,
    )(in_hbm(keys), in_hbm(values))
    chunk = (first, *rest)
    a0 = send(chunk[0], ring2)
    s = send(chunk[3], pair)
    a1 = send(chunk[1], ring2)
    a2 = send(chunk[2], ring2)
    x0 = send(pick(a0, chunk[0]), pair)
    f = send(pick(chunk[3], s), ring2)
    x1 = send(pick(a1, chunk[1]), pair)
    a3 = send(chunk[3], shift2)
    x2 = send(pick(a2, chunk[2]), pair)

    flops = 3 * 4 * tok * tok * width

    cost = pl.CostEstimate(flops=flops, bytes_accessed=tok * width * 20, transcendentals=3 * tok * tok * 2)
    att_shape = jax.ShapeDtypeStruct((tok, width), jnp.bfloat16)
    acc_shape = jax.ShapeDtypeStruct((tok, width), jnp.float32)
    stat_shape = jax.ShapeDtypeStruct((2 * (width // HEAD_DIM), tok, HEAD_DIM), jnp.float32)

    def call(kernel, c, outs, operands):
        return pl.pallas_call(
            functools.partial(kernel, c),
            out_shape=outs,
            out_specs=(vmem, vmem),
            in_specs=[smem] + [vmem] * len(operands),
            compiler_params=small,
            cost_estimate=cost,
        )(me1, *operands)

    att, sq = [], []
    for c, (near, far) in enumerate(((x0, a0), (x1, a1), (x2, a2))):
        outs = (att_shape, jax.ShapeDtypeStruct((tok, HEAD_DIM), jnp.float32))
        o, q = call(attend_kernel, c, outs, (queries, chunk[c], aux, x0, a0, near, far))
        att.append(o)
        sq.append(q)
    c = CHUNKS - 1
    state = call(partial_kernel, c, (acc_shape, stat_shape), (queries, chunk[c], aux, x0, a0, s, f))
    outs = (att_shape, jax.ShapeDtypeStruct((8, tok), jnp.float32))
    o, q = call(last_kernel, c, outs, (queries, aux, a0, a3, *state, *sq))
    att.append(o)
    tp = lax.axis_size("tp")
    other = lax.ppermute(q, "tp", [(i, i ^ 1) for i in range(tp)])
    return pl.pallas_call(
        functools.partial(finish_kernel, float(feat * tp)),
        out_shape=jax.ShapeDtypeStruct((tok, feat), jnp.bfloat16),
        in_specs=[vmem] * (4 + CHUNKS),
        out_specs=hbm,
        scratch_shapes=[pltpu.VMEM((tok, feat), jnp.bfloat16), pltpu.SemaphoreType.DMA((FINISH_BLOCKS,))],
        name="finish",
        compiler_params=small,
    )(q, other, aux, norm_gain, *att)


def solution(mesh):
    return jax.shard_map(
        on_device,
        mesh=mesh,
        in_specs=(
            P(("grp", "seq"), "tp"),
            P(("grp", "seq"), "tp"),
            P(("grp", "seq"), "tp"),
            P(("grp", "seq")),
            P(("grp", "seq")),
            P(None, "tp"),
        ),
        out_specs=P(("grp", "seq"), "tp"),
        check_vma=False,
    )
```
